32 devices in a mesh: groups: 2 (over y), req: 4 (over z), head: 2 (over x), pair: 2 (over core).
Axes of the slice: x: 2, y: 2, z: 4, core: 2. Of those that a mesh axis runs over, the one named last changes fastest.
Arguments:
- query: bfloat16 [256, 8192], P(('groups', 'req', 'pair'), 'head'), parts along dimension 0, may hold values from -80 to 80
- new_keys: bfloat16 [256, 512], P(('groups', 'req', 'pair'), 'head'), parts along dimension 0, may hold values from -4 to 4
- new_values: bfloat16 [256, 512], P(('groups', 'req', 'pair'), 'head'), parts along dimension 0, may hold values from -4 to 4
- key_cache: bfloat16 [256, 512, 512], P(('groups', 'req', 'pair'), None, 'head'), parts along dimension 0, may hold values from -4 to 4
- value_cache: bfloat16 [256, 512, 512], P(('groups', 'req', 'pair'), None, 'head'), parts along dimension 0, may hold values from -4 to 4
- lengths: int32 [256], P(('groups', 'req', 'pair')), parts along dimension 0, may hold values from 1 to 512, as said below
- residual: bfloat16 [256, 8192], P(('groups', 'req', 'pair'), 'head'), parts along dimension 0, may hold values from -1.6 to 1.6
- norm_gain: float32 [8192], P('head'), may hold values from 0.5 to 1.5
- gate_weight: bfloat16 [26624, 8192], P(('req', 'pair'), 'head'), may hold values from -0.0625 to 0.0625
- up_weight: bfloat16 [26624, 8192], P(('req', 'pair'), 'head'), may hold values from -0.0625 to 0.0625
- down_weight: bfloat16 [26624, 8192], P(('req', 'pair'), 'head'), may hold values from -0.0390625 to 0.0390625
Outputs:
- mixed: bfloat16 [256, 8192], P(('groups', 'req', 'pair'), 'head'), parts along dimension 0
The draws below stay inside these ranges and needn't reach their ends.
There are 2 independent parts, one for each index of `groups`. The reference program is written for one: setup_inputs(seed, part) draws one part's arguments, and reference() takes and returns one part's arrays. A program takes and returns all parts, laid end to end along the dimension named above; an argument that names none is the same for every part. Nothing has to cross between parts.
Inputs may be any that keep to these rules, and one draw needn't show every extreme that they name: `lengths`: every row has at least one cached position in use; in every draw some row uses all 512.
All inputs are finite; a program needn't handle non-finite values.
Results may differ from the reference program's by a relative error of at most 0.023.
Values may be sent and summed in bfloat16 or wider, within the bound.
No kernel may reach another device: no remote copies, remote signals or barrier semaphores. Data moves between devices by JAX's collectives and lax.ppermute only.
A program may use at most 192 MiB of HBM per device.

```python
import math
import jax
import jax.numpy as jnp
from jax import lax

HEAD_DIM = 128
HEADS = 64
KV_HEADS = 4
GROUP = 16
D = 8192
FF = 26624
CACHE = 512
SLOT_DEV = 16
SLOTS = 128


def shared_keys(key):
    shared = jax.random.normal(jax.random.fold_in(key, 101), (SLOTS, KV_HEADS * HEAD_DIM), jnp.float32)
    return jnp.clip(shared, -4.0, 4.0)


def draw_new_keys(key, part):
    return shared_keys(key).astype(jnp.bfloat16)


def draw_query(key, part):
    result = jnp.clip(jax.random.normal(jax.random.fold_in(key, 1), (SLOTS, HEADS, HEAD_DIM), jnp.float32), -4.0, 4.0)
    return result.reshape(SLOTS, HEADS * HEAD_DIM).astype(jnp.bfloat16)


def draw_key_cache(key, part):
    full_shape = (SLOTS, CACHE, KV_HEADS * HEAD_DIM)
    result = jnp.clip(jax.random.normal(jax.random.fold_in(key, 1), full_shape, jnp.float32), -4.0, 4.0)
    return result.astype(jnp.bfloat16)


def draw_residual(key, part):
    columns = jnp.arange(D, dtype=jnp.float32) / D
    entries = jnp.clip(jax.random.normal(jax.random.fold_in(key, 1), (SLOTS, D), jnp.float32), -4.0, 4.0)
    result = 0.1 * entries * jnp.sqrt(1.0 + 2.0 * columns)[None, :]
    return result.astype(jnp.bfloat16)


def draw_lengths(key, part):
    devices_count = SLOTS // SLOT_DEV
    limits = jax.random.randint(jax.random.fold_in(key, 1), (devices_count, 1), CACHE // 4, CACHE + 1)
    raw_bits = jax.random.randint(jax.random.fold_in(key, 2), (devices_count, SLOT_DEV), 0, 1 << 20)
    picked = (1 + raw_bits % limits).reshape(SLOTS)
    target = jax.random.randint(jax.random.fold_in(key, 3), (), 0, SLOTS)
    return picked.at[target].set(CACHE).astype(jnp.int32)


def steps_of(stream_key, extent, cuts, smallest, largest):
    def one(axis_at, shards_of):
        draws = jax.random.uniform(jax.random.fold_in(jax.random.fold_in(stream_key, 6), axis_at), (shards_of,), jnp.float32, smallest / len(cuts), largest / len(cuts))
        return jnp.repeat(jnp.exp(draws), extent[axis_at] // shards_of).reshape((-1,) + (1,) * (len(extent) - axis_at - 1))

    factor_of = one(*cuts[0])
    for cut in cuts[1:]:
        factor_of = factor_of * one(*cut)
    return factor_of


def scatter_about(key, extent, deviation, reach, pieces=(), kind=jnp.bfloat16):
    values = jax.random.normal(key, extent, jnp.float32) * deviation
    if len(pieces) > 0:
        values = steps_of(key, extent, pieces, -0.22, 0.18) * values
    return jnp.clip(values, min=-reach, max=reach).astype(kind)


def setup_inputs(seed: int = 0, part: int = 0) -> dict:
    splits = jax.random.split(jax.random.key(seed), 12)
    own_keys = jax.random.split(jax.random.fold_in(splits[11], part), 12)
    query = draw_query(jax.random.fold_in(jax.random.fold_in(splits[11], part), 71), part)
    new_keys = draw_new_keys(jax.random.fold_in(jax.random.fold_in(splits[11], part), 71), part)
    new_values = scatter_about(own_keys[2], (SLOTS, KV_HEADS * HEAD_DIM), 1.0, 4.0, ((0, 8), (1, 2)))
    key_cache = draw_key_cache(jax.random.fold_in(jax.random.fold_in(splits[11], part), 71), part)
    value_cache = scatter_about(own_keys[4], (SLOTS, CACHE, KV_HEADS * HEAD_DIM), 1.0, 4.0, ((0, 8), (2, 2)))
    lengths = draw_lengths(jax.random.fold_in(jax.random.fold_in(splits[11], part), 71), part)
    residual = draw_residual(jax.random.fold_in(jax.random.fold_in(splits[11], part), 71), part)
    norm_gain = jnp.clip(1.0 + 0.1 * jax.random.normal(splits[7], (D,), jnp.float32), 0.5, 1.5)
    gate_weight = scatter_about(splits[8], (FF, D), D ** -0.5, 0.0625, ((0, 8), (1, 2)))
    up_weight = scatter_about(splits[9], (FF, D), D ** -0.5, 0.0625, ((0, 8), (1, 2)))
    down_weight = scatter_about(splits[10], (FF, D), FF ** -0.5, 0.0390625, ((0, 8), (1, 2)))
    return {"query": query, "new_keys": new_keys, "new_values": new_values, "key_cache": key_cache, "value_cache": value_cache, "lengths": lengths, "residual": residual, "norm_gain": norm_gain, "gate_weight": gate_weight, "up_weight": up_weight, "down_weight": down_weight}


highest = lax.Precision.HIGHEST
contract_last = (((1,), (1,)), ((), ()))

def attend_row(inputs):
    query_row, key_new, value_new, key_rows, value_rows, length = inputs
    query_heads = query_row.astype(jnp.float32).reshape(KV_HEADS, GROUP, HEAD_DIM)
    key_heads = key_rows.astype(jnp.float32).reshape(CACHE, KV_HEADS, HEAD_DIM)
    value_heads = value_rows.astype(jnp.float32).reshape(CACHE, KV_HEADS, HEAD_DIM)
    own_key = key_new.astype(jnp.float32).reshape(KV_HEADS, HEAD_DIM)
    own_value = value_new.astype(jnp.float32).reshape(KV_HEADS, HEAD_DIM)
    score_scale = 1.0 / math.sqrt(HEAD_DIM)
    scores = jnp.einsum('gjd,tgd->gjt', query_heads, key_heads, precision=highest) * score_scale
    own_score = jnp.einsum('gjd,gd->gj', query_heads, own_key, precision=highest) * score_scale
    is_live = (jnp.arange(CACHE) < length)[None, None, :]
    row_max = jnp.maximum(lax.optimization_barrier(jnp.max(jnp.where(is_live, scores, -jnp.inf), axis=2)), own_score)
    weights = jnp.where(is_live, jnp.exp(scores - row_max[:, :, None]), 0.0)
    own_weight = jnp.exp(own_score - row_max)
    weight_sum = lax.optimization_barrier(jnp.sum(weights, axis=2)) + own_weight
    summed = jnp.einsum('gjt,tgd->gjd', weights, value_heads, precision=highest)
    summed = summed + own_weight[:, :, None] * own_value[:, None, :]
    return (summed / weight_sum[:, :, None]).reshape(HEADS * HEAD_DIM)

def reference(query, new_keys, new_values, key_cache, value_cache, lengths, residual, norm_gain, gate_weight, up_weight, down_weight):
    attention = lax.map(attend_row, (query, new_keys, new_values, key_cache, value_cache, lengths))
    stream = residual.astype(jnp.float32) + attention
    mean_square = lax.optimization_barrier(jnp.mean(stream * stream, axis=1, keepdims=True))
    normed = (stream * lax.rsqrt(mean_square + 1e-05) * norm_gain).astype(jnp.bfloat16)
    gate_out = lax.dot_general(normed, gate_weight, contract_last, preferred_element_type=jnp.float32)
    up_out = lax.dot_general(normed, up_weight, contract_last, preferred_element_type=jnp.float32)
    hidden = (jax.nn.silu(gate_out) * up_out).astype(jnp.bfloat16)
    ffn_out = jnp.dot(hidden, down_weight, preferred_element_type=jnp.float32)
    return (stream + ffn_out).astype(jnp.bfloat16)
```

```python
import functools
import math

import jax
import jax.numpy as jnp
from jax import lax
from jax.experimental import pallas as pl
from jax.experimental.pallas import tpu as pltpu
from jax.sharding import PartitionSpec as P

HEAD_DIM = 128
GROUP = 16
LOW = -1e30
STAT = 128

contract_last = (((1,), (1,)), ((), ()))
contract_first = (((0,), (0,)), ((), ()))
ANY = pl.BlockSpec(memory_space=pl.ANY)
VMEM = pl.BlockSpec(memory_space=pltpu.VMEM)
SMEM = pl.BlockSpec(memory_space=pltpu.SMEM)


def split3(v):
    hi = v.astype(jnp.bfloat16)
    rest = v - hi.astype(jnp.float32)
    mid = rest.astype(jnp.bfloat16)
    low = (rest - mid.astype(jnp.float32)).astype(jnp.bfloat16)
    return hi, mid, low


def attend_kernel(
    lengths, q_ref, nk_ref, nv_ref, k_ref, v_ref, res_ref, gain_ref, stream_ref, y_ref, qs, os_, nk, nv, *, block
):
    step = pl.program_id(0)
    rows, width = q_ref.shape
    heads = width // HEAD_DIM
    cache = k_ref.shape[1]
    kv = k_ref.shape[2] // HEAD_DIM
    scale = 1.0 / math.sqrt(HEAD_DIM)

    @pl.when(step == 0)
    def _():
        for j in range(heads):
            qs[pl.ds(j, rows, stride=heads), :] = q_ref[:, j * HEAD_DIM : (j + 1) * HEAD_DIM].astype(
                jnp.float32
            )

        for g in range(kv):
            lanes = slice(g * HEAD_DIM, (g + 1) * HEAD_DIM)
            nk[pl.ds(g, rows, stride=kv), :] = nk_ref[:, lanes].astype(jnp.float32)
            nv[pl.ds(g, rows, stride=kv), :] = nv_ref[:, lanes].astype(jnp.float32)

    column = lax.broadcasted_iota(jnp.int32, (1, cache), 1)
    for b in range(block):
        row = step * block + b
        live = column < lengths[row]
        for g in range(kv):
            at = pl.multiple_of(row * heads + g * GROUP, GROUP)
            lanes = slice(g * HEAD_DIM, (g + 1) * HEAD_DIM)
            q = qs[pl.ds(at, GROUP), :]
            s = lax.dot_general(
                q.astype(jnp.bfloat16),
                k_ref[b, :, lanes],
                contract_last,
                preferred_element_type=jnp.float32,
            )
            s = jnp.where(live, s * scale, LOW)
            own = jnp.sum(q * nk[pl.ds(row * kv + g, 1), :], axis=1, keepdims=True) * scale
            top = jnp.maximum(jnp.max(s, axis=1, keepdims=True), own)
            w = jnp.where(live, jnp.exp(s - top), 0.0)
            own_w = jnp.exp(own - top)
            total = jnp.sum(w, axis=1, keepdims=True) + own_w
            acc = jnp.dot(w.astype(jnp.bfloat16), v_ref[b, :, lanes], preferred_element_type=jnp.float32)
            acc = acc + own_w * nv[pl.ds(row * kv + g, 1), :]
            os_[pl.ds(at, GROUP), :] = acc / total

    @pl.when(step == pl.num_programs(0) - 1)
    def _():
        squares = jnp.zeros((rows, HEAD_DIM), jnp.float32)
        for j in range(heads):
            lanes = slice(j * HEAD_DIM, (j + 1) * HEAD_DIM)
            stream = res_ref[:, lanes].astype(jnp.float32) + os_[pl.ds(j, rows, stride=heads), :]
            stream_ref[:, lanes] = stream
            squares = squares + stream * stream
            y_ref[:, lanes] = (stream * gain_ref[:, lanes]).astype(jnp.bfloat16)
        hi, mid, low = split3(jnp.sum(squares, axis=1, keepdims=True))
        lane = lax.broadcasted_iota(jnp.int32, (rows, STAT), 1)
        f = lambda v: v.astype(jnp.float32)
        stat = jnp.where(lane == 0, f(hi), jnp.where(lane == 1, f(mid), jnp.where(lane == 2, f(low), 0.0)))
        y_ref[:, width : width + STAT] = stat.astype(jnp.bfloat16)


def attend(query, new_keys, new_values, key_cache, value_cache, lengths, residual, gain):
    rows, width = query.shape
    heads = width // HEAD_DIM
    cache, kvw = key_cache.shape[1:]
    block = 4 if rows % 4 == 0 else 1
    whole = lambda shape: pl.BlockSpec(shape, lambda i, n: (0,) * len(shape))
    cache_spec = pl.BlockSpec((block, cache, kvw), lambda i, n: (i, 0, 0))
    return pl.pallas_call(
        functools.partial(attend_kernel, block=block),
        grid_spec=pltpu.PrefetchScalarGridSpec(
            num_scalar_prefetch=1,
            grid=(rows // block,),
            in_specs=[
                whole((rows, width)),
                whole(new_keys.shape),
                whole(new_values.shape),
                cache_spec,
                cache_spec,
                whole((rows, width)),
                whole((1, width)),
            ],
            out_specs=[whole((rows, width)), whole((rows, width + STAT))],
            scratch_shapes=[
                pltpu.VMEM((rows * heads, HEAD_DIM), jnp.float32),
                pltpu.VMEM((rows * heads, HEAD_DIM), jnp.float32),
                pltpu.VMEM((rows * kvw // HEAD_DIM, HEAD_DIM), jnp.float32),
                pltpu.VMEM((rows * kvw // HEAD_DIM, HEAD_DIM), jnp.float32),
            ],
        ),
        out_shape=[
            jax.ShapeDtypeStruct((rows, width), jnp.float32),
            jax.ShapeDtypeStruct((rows, width + STAT), jnp.bfloat16),
        ],
        compiler_params=pltpu.CompilerParams(vmem_limit_bytes=32 << 20),
        name="attend",
    )(lengths, query, new_keys, new_values, key_cache, value_cache, residual, gain.reshape(1, width))


def fetch(start, steps, depth, copies):
    for i in range(min(depth, steps)):
        for c in copies(i, i):
            c.start()


def units_kernel(*refs, pieces, count, tile, depth, stats, narrow):
    start, *refs = refs
    piece_refs, refs = refs[:pieces], refs[pieces:]
    gate, up, out = refs[:3]
    refs = refs[3:]
    if stats:
        stat_out, *refs = refs
    rows, gbuf, ubuf, row_sem, sems = refs
    per = piece_refs[0].shape[0]
    width = gate.shape[1]
    steps = count // tile
    first = start[0]

    def copies(i, slot):
        at = pl.multiple_of(first + i * tile, 16)
        return (
            pltpu.make_async_copy(gate.at[pl.ds(at, tile)], gbuf.at[slot], sems.at[0, slot]),
            pltpu.make_async_copy(up.at[pl.ds(at, tile)], ubuf.at[slot], sems.at[1, slot]),
        )

    gathers = [
        pltpu.make_async_copy(p, rows.at[pl.ds(i * per, per)], row_sem.at[i]) for i, p in enumerate(piece_refs)
    ]
    for c in gathers:
        c.start()
    for i in range(min(depth, steps)):
        for c in copies(i, i):
            c.start()
    for c in gathers:
        c.wait()

    if stats:
        stat = rows[:, width : width + STAT].astype(jnp.float32).T[:16]
        stat_out[...] = stat
        if narrow:
            out[2 * count : 2 * count + 16, :] = stat.astype(out.dtype)

    def body(i, _):
        slot = lax.rem(i, depth)
        for c in copies(i, slot):
            c.wait()
        at = pl.multiple_of(i * tile, 16)
        x = rows[:, :width]
        g = lax.dot_general(gbuf[slot], x, contract_last, preferred_element_type=jnp.float32)
        out[pl.ds(at, tile), :] = g.astype(out.dtype)
        u = lax.dot_general(ubuf[slot], x, contract_last, preferred_element_type=jnp.float32)
        out[pl.ds(count + at, tile), :] = u.astype(out.dtype)

        @pl.when(i + depth < steps)
        def _():
            for c in copies(i + depth, slot):
                c.start()

        return 0

    lax.fori_loop(0, steps, body, 0)


def units(start, pieces, gate, up, count, tile, stats, narrow, name):
    per, ext = pieces[0].shape
    n = len(pieces)
    rows = per * n
    width = gate.shape[1]
    depth = 3
    out_rows = 2 * count + (16 if (stats and narrow) else 0)
    out_shape = [jax.ShapeDtypeStruct((out_rows, rows), jnp.bfloat16 if narrow else jnp.float32)]
    if stats:
        out_shape.append(jax.ShapeDtypeStruct((16, rows), jnp.float32))
    return pl.pallas_call(
        functools.partial(
            units_kernel, pieces=n, count=count, tile=tile, depth=depth, stats=stats, narrow=narrow
        ),
        in_specs=[SMEM] + [ANY] * (n + 2),
        out_specs=[VMEM] * len(out_shape),
        out_shape=out_shape,
        scratch_shapes=[
            pltpu.VMEM((rows, ext), jnp.bfloat16),
            pltpu.VMEM((depth, tile, width), jnp.bfloat16),
            pltpu.VMEM((depth, tile, width), jnp.bfloat16),
            pltpu.SemaphoreType.DMA((n,)),
            pltpu.SemaphoreType.DMA((2, depth)),
        ],
        compiler_params=pltpu.CompilerParams(vmem_limit_bytes=32 << 20),
        cost_estimate=pl.CostEstimate(
            flops=4 * count * width * rows, bytes_accessed=4 * count * width, transcendentals=0
        ),
        name=name,
    )(start, *pieces, gate, up)


def down_kernel(start, *refs, parts, count, tile, depth, has_acc, last, keep):
    hidden, refs = refs[:parts], refs[parts:]
    weight, *refs = refs
    if has_acc:
        acc_in, *refs = refs
    if last:
        send, kept, acc, buf, sems = refs
    else:
        acc, buf, sems = refs
    per = count // tile
    steps = parts * per
    first = start[0]

    def copy(i, slot):
        at = pl.multiple_of(first + i * tile, 16)
        return pltpu.make_async_copy(weight.at[pl.ds(at, tile)], buf.at[slot], sems.at[slot])

    for i in range(min(depth, steps)):
        copy(i, i).start()
    if has_acc:
        acc[...] = acc_in[...]
    for p in range(parts):

        def body(i, _, p=p):
            n = p * per + i
            slot = lax.rem(n, depth)
            copy(n, slot).wait()
            at = pl.multiple_of(i * tile, 16)
            h = hidden[p][pl.ds(at, tile), :]
            part = lax.dot_general(h, buf[slot], contract_first, preferred_element_type=jnp.float32)
            if has_acc:
                acc[...] += part
            else:

                @pl.when(n == 0)
                def _():
                    acc[...] = part

                @pl.when(n > 0)
                def _():
                    acc[...] += part

            @pl.when(n + depth < steps)
            def _():
                copy(n + depth, slot).start()

            return 0

        lax.fori_loop(0, per, body, 0)
    if last:
        kept[...] = acc[:keep]
        send[...] = acc[keep:].astype(jnp.bfloat16)


def down(start, hidden, weight, acc, count, tile, keep, name):
    rows = hidden[0].shape[1]
    width = weight.shape[1]
    depth = 3
    last = keep > 0
    parts = len(hidden)
    f32 = jax.ShapeDtypeStruct((rows, width), jnp.float32)
    if last:
        out_shape = [
            jax.ShapeDtypeStruct((rows - keep, width), jnp.bfloat16),
            jax.ShapeDtypeStruct((keep, width), jnp.float32),
        ]
        acc_scratch = [pltpu.VMEM((rows, width), jnp.float32)]
    else:
        out_shape = f32
        acc_scratch = []
    extra = [] if acc is None else [acc]
    return pl.pallas_call(
        functools.partial(
            down_kernel,
            parts=parts,
            count=count,
            tile=tile,
            depth=depth,
            has_acc=acc is not None,
            last=last,
            keep=keep,
        ),
        in_specs=[SMEM] + [VMEM] * parts + [ANY] + [VMEM] * len(extra),
        out_specs=[VMEM, VMEM] if last else VMEM,
        out_shape=out_shape,
        scratch_shapes=acc_scratch
        + [pltpu.VMEM((depth, tile, width), jnp.bfloat16), pltpu.SemaphoreType.DMA((depth,))],
        compiler_params=pltpu.CompilerParams(vmem_limit_bytes=32 << 20),
        cost_estimate=pl.CostEstimate(
            flops=2 * parts * count * width * rows,
            bytes_accessed=2 * parts * count * width,
            transcendentals=0,
        ),
        name=name,
    )(start, *hidden, weight, *extra)


def tile_of(count, most):
    return max(t for t in range(16, most + 1, 16) if count % t == 0)


def solution(mesh):
    n_req, n_head, n_pair = (mesh.shape[a] for a in ("req", "head", "pair"))

    def shift(x, axis, by):
        n = mesh.shape[axis]
        return lax.ppermute(x, axis, [(i, (i + by) % n) for i in range(n)])

    def local(
        query,
        new_keys,
        new_values,
        key_cache,
        value_cache,
        lengths,
        residual,
        norm_gain,
        gate_weight,
        up_weight,
        down_weight,
    ):
        slot_rows, width = query.shape
        features = width * n_head
        stream, y = attend(
            query, new_keys, new_values, key_cache, value_cache, lengths, residual, norm_gain
        )
        near = [y] + [shift(y, "req", -s) for s in range(1, n_req)]
        pieces = list(near)
        for p in range(1, n_pair):
            pieces += [shift(b, "pair", -p) for b in near]
        rows = slot_rows * len(pieces)

        unit_count = gate_weight.shape[0]
        share = unit_count // n_head
        chunks = 2 if (share // 2) % 16 == 0 else 1
        count = share // chunks
        tile = tile_of(count, 208)
        me = lax.axis_index("head")

        def begin(j, k):
            return (lax.rem(me + j, n_head) * share + k * count).reshape(1)

        received = [[] for _ in range(chunks)]
        stat_own = None
        for k in range(chunks):
            for j in range(1, n_head):
                first = k == 0
                out = units(
                    begin(j, k), pieces, gate_weight, up_weight, count, tile, first, True, f"send{k}_{j}"
                )
                if first:
                    stat_own = out[1]
                received[k].append(shift(out[0], "head", j))
        stat = stat_own[0] + stat_own[1] + stat_own[2]
        for r in received[0]:
            tail = r[2 * count : 2 * count + 3].astype(jnp.float32)
            stat = stat + (tail[0] + tail[1] + tail[2])
        inverse = lax.rsqrt(stat / features + 1e-05)[None, :]

        (mine,) = units(begin(0, 0), pieces, gate_weight, up_weight, share, tile, False, False, "keep")
        hidden = []
        for k in range(chunks):
            gate = mine[k * count : (k + 1) * count]
            up = mine[share + k * count : share + (k + 1) * count]
            for r in received[k]:
                gate = gate + r[:count].astype(jnp.float32)
                up = up + r[count : 2 * count].astype(jnp.float32)
            hidden.append((jax.nn.silu(gate * inverse) * (up * inverse)).astype(jnp.bfloat16))
        others = [[shift(h, "head", j) for h in hidden] for j in range(1, n_head)]

        keep = rows // n_pair
        down_tile = tile_of(count, 416)
        acc = down(begin(0, 0), hidden, down_weight, None, count, down_tile, 0, "down_own")
        for k in range(chunks):
            for j in range(1, n_head):
                last = k == chunks - 1 and j == n_head - 1
                acc = down(
                    begin(n_head - j, k),
                    [others[j - 1][k]],
                    down_weight,
                    acc,
                    count,
                    down_tile,
                    keep if last else 0,
                    f"down{k}_{j}",
                )
        send, kept = acc
        total = kept
        for p in range(1, n_pair):
            part = send[(p - 1) * keep : p * keep]
            total = total + shift(part, "pair", p).astype(jnp.float32)
        result = stream + total[:slot_rows]
        for s in range(1, n_req):
            part = total[s * slot_rows : (s + 1) * slot_rows].astype(jnp.bfloat16)
            result = result + shift(part, "req", s).astype(jnp.float32)
        return result.astype(jnp.bfloat16)

    rows_spec = P(("groups", "req", "pair"), "head")
    return jax.shard_map(
        local,
        mesh=mesh,
        in_specs=(
            rows_spec,
            rows_spec,
            rows_spec,
            P(("groups", "req", "pair"), None, "head"),
            P(("groups", "req", "pair"), None, "head"),
            P(("groups", "req", "pair")),
            rows_spec,
            P("head"),
            P(("req", "pair"), "head"),
            P(("req", "pair"), "head"),
            P(("req", "pair"), "head"),
        ),
        out_specs=rows_spec,
        check_vma=False,
    )
```

```python
import functools
import math

import jax
import jax.numpy as jnp
from jax import lax
from jax.experimental import pallas as pl
from jax.experimental.pallas import tpu as pltpu
from jax.sharding import PartitionSpec as P

HEAD_DIM = 128
GROUP = 16
LOW = -1e30
STAT = 128

contract_last = (((1,), (1,)), ((), ()))
contract_first = (((0,), (0,)), ((), ()))
ANY = pl.BlockSpec(memory_space=pl.ANY)
HBM = pl.BlockSpec(memory_space=pltpu.HBM)
VMEM = pl.BlockSpec(memory_space=pltpu.VMEM)
SMEM = pl.BlockSpec(memory_space=pltpu.SMEM)


def split3(v):
    hi = v.astype(jnp.bfloat16)
    rest = v - hi.astype(jnp.float32)
    mid = rest.astype(jnp.bfloat16)
    low = (rest - mid.astype(jnp.float32)).astype(jnp.bfloat16)
    return hi, mid, low


def attend_kernel(
    lengths_hbm, q_hbm, nk_hbm, nv_hbm, k_hbm, v_hbm, res_hbm, gain_hbm, stream_ref, y_ref,
    q_ref, nk_ref, nv_ref, kb, vb, res_ref, gain_ref, lengths, qs, os_, small, sems, *, block,
):
    rows, width = q_ref.shape
    heads = width // HEAD_DIM
    cache, lanes_kv = kb.shape[1:]
    kv = lanes_kv // HEAD_DIM
    scale = 1.0 / math.sqrt(HEAD_DIM)
    first = [(lengths_hbm, lengths), (q_hbm, q_ref), (nk_hbm, nk_ref), (nv_hbm, nv_ref)]
    late = [(res_hbm, res_ref), (gain_hbm, gain_ref)]
    smalls = [pltpu.make_async_copy(s, d, small.at[i]) for i, (s, d) in enumerate(first + late)]
    caches = [
        [
            pltpu.make_async_copy(h.at[pl.ds(i * block, block)], d.at[pl.ds(i * block, block)], sems.at[j, i])
            for j, (h, d) in enumerate(((k_hbm, kb), (v_hbm, vb)))
        ]
        for i in range(rows // block)
    ]
    for c in smalls[:4]:
        c.start()
    for pair in caches:
        for c in pair:
            c.start()
    for c in smalls[4:]:
        c.start()
    for c in smalls[:4]:
        c.wait()
    for j in range(heads):
        qs[pl.ds(j, rows, stride=heads), :] = q_ref[:, j * HEAD_DIM : (j + 1) * HEAD_DIM].astype(jnp.float32)

    column = lax.broadcasted_iota(jnp.int32, (1, cache), 1)
    same = (
        lax.broadcasted_iota(jnp.int32, (heads, lanes_kv), 0) // GROUP
        == lax.broadcasted_iota(jnp.int32, (heads, lanes_kv), 1) // HEAD_DIM
    )
    for i in range(rows // block):
        for c in caches[i]:
            c.wait()
        scores = []
        for row in range(i * block, (i + 1) * block):
            q = qs[row * heads : (row + 1) * heads, :]
            q = jnp.where(same, jnp.concatenate([q] * kv, axis=1), 0.0)
            own = jnp.sum(q * nk_ref[row : row + 1, :].astype(jnp.float32), axis=1, keepdims=True) * scale
            s = lax.dot_general(
                q.astype(jnp.bfloat16), kb[row], contract_last, preferred_element_type=jnp.float32
            )
            scores.append((s * scale, own))
        weights = []
        for b, (s, own) in enumerate(scores):
            live = column < lengths[i * block + b]
            s = jnp.where(live, s, LOW)
            top = jnp.maximum(jnp.max(s, axis=1, keepdims=True), own)
            w = jnp.where(live, jnp.exp(s - top), 0.0)
            own_w = jnp.exp(own - top)
            weights.append((w.astype(jnp.bfloat16), own_w, jnp.sum(w, axis=1, keepdims=True) + own_w))
        for b, (w, own_w, total) in enumerate(weights):
            row = i * block + b
            acc = jnp.dot(w, vb[row], preferred_element_type=jnp.float32)
            acc = (acc + own_w * nv_ref[row : row + 1, :].astype(jnp.float32)) / total
            for g in range(kv):
                heads_g = slice(g * GROUP, (g + 1) * GROUP)
                os_[row * heads + g * GROUP : row * heads + (g + 1) * GROUP, :] = acc[
                    heads_g, g * HEAD_DIM : (g + 1) * HEAD_DIM
                ]

    for c in smalls[4:]:
        c.wait()
    squares = jnp.zeros((rows, HEAD_DIM), jnp.float32)
    for j in range(heads):
        lanes = slice(j * HEAD_DIM, (j + 1) * HEAD_DIM)
        stream = res_ref[:, lanes].astype(jnp.float32) + os_[pl.ds(j, rows, stride=heads), :]
        stream_ref[:, lanes] = stream
        squares = squares + stream * stream
        y_ref[:, lanes] = (stream * gain_ref[:, lanes]).astype(jnp.bfloat16)
    hi, mid, low = split3(jnp.sum(squares, axis=1, keepdims=True))
    lane = lax.broadcasted_iota(jnp.int32, (rows, STAT), 1)
    f = lambda v: v.astype(jnp.float32)
    stat = jnp.where(lane == 0, f(hi), jnp.where(lane == 1, f(mid), jnp.where(lane == 2, f(low), 0.0)))
    y_ref[:, width : width + STAT] = stat.astype(jnp.bfloat16)


def attend(query, new_keys, new_values, key_cache, value_cache, lengths, residual, gain):
    rows, width = query.shape
    heads = width // HEAD_DIM
    block = 4
    gain = gain.reshape(1, width)
    arrays = (query, new_keys, new_values, key_cache, value_cache, residual, gain)
    in_hbm = [pltpu.with_memory_space_constraint(a, pltpu.HBM) for a in (lengths, *arrays)]
    return pl.pallas_call(
        functools.partial(attend_kernel, block=block),
        in_specs=[HBM] * len(in_hbm),
        out_specs=[VMEM, VMEM],
        out_shape=[
            jax.ShapeDtypeStruct((rows, width), jnp.float32),
            jax.ShapeDtypeStruct((rows, width + STAT), jnp.bfloat16),
        ],
        scratch_shapes=[pltpu.VMEM(a.shape, a.dtype) for a in arrays]
        + [
            pltpu.SMEM(lengths.shape, lengths.dtype),
            pltpu.VMEM((rows * heads, HEAD_DIM), jnp.float32),
            pltpu.VMEM((rows * heads, HEAD_DIM), jnp.float32),
            pltpu.SemaphoreType.DMA((6,)),
            pltpu.SemaphoreType.DMA((2, rows // block)),
        ],
        compiler_params=pltpu.CompilerParams(vmem_limit_bytes=32 << 20),
        name="attend",
    )(*in_hbm)


def units_kernel(*refs, pieces, count, tile, depth, stats, narrow):
    start, *refs = refs
    piece_refs, refs = refs[:pieces], refs[pieces:]
    gate, up, out = refs[:3]
    refs = refs[3:]
    if stats:
        stat_out, *refs = refs
    if narrow:
        acc, *refs = refs
    else:
        acc = out
    gbuf, ubuf, sems = refs
    width = gate.shape[1]
    steps = width // tile
    first = pl.multiple_of(start[0], 16)

    def copies(i):
        return [
            pltpu.make_async_copy(
                w.at[pl.ds(first, count), pl.ds(i * tile, tile)], b.at[i % depth], sems.at[j, i % depth]
            )
            for j, (w, b) in enumerate(((gate, gbuf), (up, ubuf)))
        ]

    for i in range(min(depth, steps)):
        for c in copies(i):
            c.start()
    if stats:
        stat = jnp.concatenate([p[:, width : width + STAT] for p in piece_refs], axis=0)
        stat = stat.astype(jnp.float32).T[:16]
        stat_out[...] = stat
        if narrow:
            out[2 * count : 2 * count + 16, :] = stat.astype(out.dtype)
    for i in range(steps):
        for c in copies(i):
            c.wait()
        x = jnp.concatenate([p[:, i * tile : (i + 1) * tile] for p in piece_refs], axis=0)
        for j, b in enumerate((gbuf, ubuf)):
            part = lax.dot_general(b[i % depth], x, contract_last, preferred_element_type=jnp.float32)
            at = slice(j * count, (j + 1) * count)
            if i > 0:
                part = acc[at] + part
            if i < steps - 1:
                acc[at] = part
            else:
                out[at] = part.astype(out.dtype)
        if i + depth < steps:
            for c in copies(i + depth):
                c.start()


def units(start, pieces, gate, up, count, stats, narrow, name):
    rows = sum(p.shape[0] for p in pieces)
    n = len(pieces)
    width = gate.shape[1]
    tile = min(512, width)
    depth = min(width // tile, max(2, (14 << 20) // (4 * count * tile)))
    out_rows = 2 * count + (16 if (stats and narrow) else 0)
    out_shape = [jax.ShapeDtypeStruct((out_rows, rows), jnp.bfloat16 if narrow else jnp.float32)]
    if stats:
        out_shape.append(jax.ShapeDtypeStruct((16, rows), jnp.float32))
    return pl.pallas_call(
        functools.partial(
            units_kernel, pieces=n, count=count, tile=tile, depth=depth, stats=stats, narrow=narrow
        ),
        in_specs=[SMEM] + [VMEM] * n + [ANY] * 2,
        out_specs=[VMEM] * len(out_shape),
        out_shape=out_shape,
        scratch_shapes=([pltpu.VMEM((2 * count, rows), jnp.float32)] if narrow else [])
        + [
            pltpu.VMEM((depth, count, tile), jnp.bfloat16),
            pltpu.VMEM((depth, count, tile), jnp.bfloat16),
            pltpu.SemaphoreType.DMA((2, depth)),
        ],
        compiler_params=pltpu.CompilerParams(vmem_limit_bytes=36 << 20),
        cost_estimate=pl.CostEstimate(
            flops=4 * count * width * rows, bytes_accessed=4 * count * width, transcendentals=0
        ),
        name=name,
    )(start, *pieces, gate, up)


def down_kernel(start, *refs, parts, tile, has_acc, last, keep, offset):
    hidden, refs = refs[:parts], refs[parts:]
    weight, *refs = refs
    if has_acc:
        acc, *refs = refs
    if last:
        send, kept, *refs = refs
    else:
        out, *refs = refs
    turned, buf, sems = refs
    steps, units_in = buf.shape[:2]
    count = units_in // parts
    first = pl.multiple_of(start[0], 16)

    copies = [
        pltpu.make_async_copy(
            weight.at[pl.ds(first, units_in), pl.ds(offset + i * tile, tile)], buf.at[i], sems.at[i]
        )
        for i in range(steps)
    ]
    for c in copies:
        c.start()
    whole = jnp.concatenate([h[...] for h in hidden], axis=0) if parts > 1 else hidden[0][...]
    turned[...] = whole.T
    for i in range(steps):
        copies[i].wait()
        lanes = slice(i * tile, (i + 1) * tile)
        part = jnp.dot(turned[...], buf[i], preferred_element_type=jnp.float32)
        if has_acc:
            part = acc[:, offset + i * tile : offset + (i + 1) * tile] + part
        if last:
            kept[:, lanes] = part[:keep]
            send[:, lanes] = part[keep:].astype(jnp.bfloat16)
        else:
            out[:, lanes] = part


def down(start, hidden, weight, acc, keep, name, offset=0, width=None):
    count, rows = hidden[0].shape
    width = width or weight.shape[1]
    tile = min(512, width)
    last = keep > 0
    parts = len(hidden)
    total = parts * count
    if last:
        out_shape = [
            jax.ShapeDtypeStruct((rows - keep, width), jnp.bfloat16),
            jax.ShapeDtypeStruct((keep, width), jnp.float32),
        ]
    else:
        out_shape = jax.ShapeDtypeStruct((rows, width), jnp.float32)
    extra = [] if acc is None else [acc]
    return pl.pallas_call(
        functools.partial(
            down_kernel, parts=parts, tile=tile, has_acc=acc is not None, last=last, keep=keep, offset=offset
        ),
        in_specs=[SMEM] + [VMEM] * parts + [ANY] + [VMEM] * len(extra),
        out_specs=[VMEM, VMEM] if last else VMEM,
        out_shape=out_shape,
        scratch_shapes=[
            pltpu.VMEM((rows, total), jnp.bfloat16),
            pltpu.VMEM((width // tile, total, tile), jnp.bfloat16),
            pltpu.SemaphoreType.DMA((width // tile,)),
        ],
        compiler_params=pltpu.CompilerParams(vmem_limit_bytes=36 << 20),
        cost_estimate=pl.CostEstimate(
            flops=2 * total * width * rows, bytes_accessed=2 * total * width, transcendentals=0
        ),
        name=name,
    )(start, *hidden, weight, *extra)


def combine_kernel(*refs, near):
    kept, *refs = refs
    received, outs = refs[:near], refs[near:]
    size = outs[0].shape[0]
    for s, out in enumerate(outs):
        at = slice(s * size, (s + 1) * size)
        total = kept[at]
        for r in received:
            total = total + r[at].astype(jnp.float32)
        out[...] = total.astype(out.dtype)


def combine(kept, received, size):
    blocks, width = kept.shape[0] // size, kept.shape[1]
    return pl.pallas_call(
        functools.partial(combine_kernel, near=len(received)),
        in_specs=[VMEM] * (1 + len(received)),
        out_specs=[VMEM] * blocks,
        out_shape=[
            jax.ShapeDtypeStruct((size, width), jnp.bfloat16 if s else jnp.float32) for s in range(blocks)
        ],
        compiler_params=pltpu.CompilerParams(vmem_limit_bytes=24 << 20),
        name="combine",
    )(kept, *received)


def solution(mesh):
    n_req, n_head, n_pair = (mesh.shape[a] for a in ("req", "head", "pair"))

    def shift(x, axis, by):
        n = mesh.shape[axis]
        return lax.ppermute(x, axis, [(i, (i + by) % n) for i in range(n)])

    order = sorted(range(1, n_req), key=lambda s: min(s, n_req - s))

    def local(
        query,
        new_keys,
        new_values,
        key_cache,
        value_cache,
        lengths,
        residual,
        norm_gain,
        gate_weight,
        up_weight,
        down_weight,
    ):
        slot_rows, width = query.shape
        features = width * n_head
        stream, y = attend(
            query, new_keys, new_values, key_cache, value_cache, lengths, residual, norm_gain
        )
        moved = {s: shift(y, "req", -s) for s in order}
        near = [y] + [moved[s] for s in range(1, n_req)]
        pieces = list(near)
        for p in range(1, n_pair):
            pieces += [shift(b, "pair", -p) for b in near]
        rows = slot_rows * len(pieces)

        unit_count = gate_weight.shape[0]
        share = unit_count // n_head
        chunks = 2 if (share // 2) % 16 == 0 else 1
        count = share // chunks
        me = lax.axis_index("head")

        def begin(j, k):
            return (lax.rem(me + j, n_head) * share + k * count).reshape(1)

        received = [[] for _ in range(chunks)]
        stat_own = None
        for k in range(chunks):
            for j in range(1, n_head):
                first = k == 0
                out = units(
                    begin(j, k), pieces, gate_weight, up_weight, count, first, True, f"send{k}_{j}"
                )
                if first:
                    stat_own = out[1]
                received[k].append(shift(out[0], "head", j))
        stat = stat_own[0] + stat_own[1] + stat_own[2]
        for r in received[0]:
            tail = r[2 * count : 2 * count + 3].astype(jnp.float32)
            stat = stat + (tail[0] + tail[1] + tail[2])
        inverse = lax.rsqrt(stat / features + 1e-05)[None, :]

        (mine,) = units(begin(0, 0), pieces, gate_weight, up_weight, share, False, False, "keep")
        hidden = []
        for k in range(chunks):
            gate = mine[k * count : (k + 1) * count]
            up = mine[share + k * count : share + (k + 1) * count]
            for r in received[k]:
                gate = gate + r[:count].astype(jnp.float32)
                up = up + r[count : 2 * count].astype(jnp.float32)
            hidden.append((jax.nn.silu(gate * inverse) * (up * inverse)).astype(jnp.bfloat16))
        others = [[shift(h, "head", j) for h in hidden] for j in range(1, n_head)]

        keep = rows // n_pair
        acc = down(begin(0, 0), hidden, down_weight, None, 0, "down_own")
        rest = [(k, j) for k in range(chunks) for j in range(1, n_head)]
        for k, j in rest[:-1]:
            acc = down(begin(n_head - j, k), [others[j - 1][k]], down_weight, acc, 0, f"down{k}_{j}")
        k, j = rest[-1]
        cuts = 1
        results = []
        for c in range(cuts):
            size = width // cuts
            send, kept = down(
                begin(n_head - j, k),
                [others[j - 1][k]],
                down_weight,
                acc,
                keep,
                f"last{c}",
                c * size,
                size,
            )
            received = [shift(send[(p - 1) * keep : p * keep], "pair", p) for p in range(1, n_pair)]
            blocks = combine(kept, received, slot_rows)
            parts = {s: shift(blocks[s], "req", s) for s in order[::-1]}
            result = stream[:, c * size : (c + 1) * size] + blocks[0]
            for s in range(1, n_req):
                result = result + parts[s].astype(jnp.float32)
            results.append(result.astype(jnp.bfloat16))
        return jnp.concatenate(results, axis=1)

    rows_spec = P(("groups", "req", "pair"), "head")
    return jax.shard_map(
        local,
        mesh=mesh,
        in_specs=(
            rows_spec,
            rows_spec,
            rows_spec,
            P(("groups", "req", "pair"), None, "head"),
            P(("groups", "req", "pair"), None, "head"),
            P(("groups", "req", "pair")),
            rows_spec,
            P("head"),
            P(("req", "pair"), "head"),
            P(("req", "pair"), "head"),
            P(("req", "pair"), "head"),
        ),
        out_specs=rows_spec,
        check_vma=False,
    )
```

```python
import functools
import math

import jax
import jax.numpy as jnp
from jax import lax
from jax.experimental import pallas as pl
from jax.experimental.pallas import tpu as pltpu
from jax.sharding import PartitionSpec as P


HEAD_DIM = 128
GROUP = 16
LOW = -1e30
STAT = 128

contract_last = (((1,), (1,)), ((), ()))
ANY = pl.BlockSpec(memory_space=pl.ANY)
HBM = pl.BlockSpec(memory_space=pltpu.HBM)
VMEM = pl.BlockSpec(memory_space=pltpu.VMEM)
SMEM = pl.BlockSpec(memory_space=pltpu.SMEM)


def split3(v):
    hi = v.astype(jnp.bfloat16)
    rest = v - hi.astype(jnp.float32)
    mid = rest.astype(jnp.bfloat16)
    low = (rest - mid.astype(jnp.float32)).astype(jnp.bfloat16)
    return hi, mid, low


def attend_kernel(
    me_ref, lengths_hbm, q_hbm, nk_hbm, nv_hbm, k_hbm, v_hbm, res_hbm, gain_hbm, stream_ref, y_ref,
    q_ref, nk_ref, nv_ref, kb, vb, res_ref, gain_ref, lengths, qs, os_, small, sems, *, block,
):
    rows, width = q_ref.shape
    heads = width // HEAD_DIM
    cache, lanes_kv = kb.shape[1:]
    kv = lanes_kv // HEAD_DIM
    scale = 1.0 / math.sqrt(HEAD_DIM)
    first = [(lengths_hbm, lengths), (q_hbm, q_ref), (nk_hbm, nk_ref), (nv_hbm, nv_ref)]
    late = [(res_hbm, res_ref), (gain_hbm, gain_ref)]
    smalls = [pltpu.make_async_copy(s, d, small.at[i]) for i, (s, d) in enumerate(first + late)]
    caches = [
        [
            pltpu.make_async_copy(h.at[pl.ds(i * block, block)], d.at[pl.ds(i * block, block)], sems.at[j, i])
            for j, (h, d) in enumerate(((k_hbm, kb), (v_hbm, vb)))
        ]
        for i in range(rows // block)
    ]
    for c in smalls[:4]:
        c.start()
    for pair in caches:
        for c in pair:
            c.start()
    for c in smalls[4:]:
        c.start()
    for c in smalls[:4]:
        c.wait()
    for j in range(heads):
        qs[pl.ds(j, rows, stride=heads), :] = q_ref[:, j * HEAD_DIM : (j + 1) * HEAD_DIM].astype(jnp.float32)

    column = lax.broadcasted_iota(jnp.int32, (1, cache), 1)
    same = (
        lax.broadcasted_iota(jnp.int32, (heads, lanes_kv), 0) // GROUP
        == lax.broadcasted_iota(jnp.int32, (heads, lanes_kv), 1) // HEAD_DIM
    )
    for i in range(rows // block):
        for c in caches[i]:
            c.wait()
        scores = []
        for row in range(i * block, (i + 1) * block):
            q = qs[row * heads : (row + 1) * heads, :]
            q = jnp.where(same, jnp.concatenate([q] * kv, axis=1), 0.0)
            own = jnp.sum(q * nk_ref[row : row + 1, :].astype(jnp.float32), axis=1, keepdims=True) * scale
            s = lax.dot_general(
                q.astype(jnp.bfloat16), kb[row], contract_last, preferred_element_type=jnp.float32
            )
            scores.append((s * scale, own))
        weights = []
        for b, (s, own) in enumerate(scores):
            live = column < lengths[i * block + b]
            s = jnp.where(live, s, LOW)
            top = jnp.maximum(jnp.max(s, axis=1, keepdims=True), own)
            w = jnp.where(live, jnp.exp(s - top), 0.0)
            own_w = jnp.exp(own - top)
            weights.append((w.astype(jnp.bfloat16), own_w, jnp.sum(w, axis=1, keepdims=True) + own_w))
        for b, (w, own_w, total) in enumerate(weights):
            row = i * block + b
            acc = jnp.dot(w, vb[row], preferred_element_type=jnp.float32)
            acc = (acc + own_w * nv_ref[row : row + 1, :].astype(jnp.float32)) / total
            for g in range(kv):
                heads_g = slice(g * GROUP, (g + 1) * GROUP)
                os_[row * heads + g * GROUP : row * heads + (g + 1) * GROUP, :] = acc[
                    heads_g, g * HEAD_DIM : (g + 1) * HEAD_DIM
                ]

    for c in smalls[4:]:
        c.wait()
    squares = jnp.zeros((rows, HEAD_DIM), jnp.float32)
    for j in range(heads):
        lanes = slice(j * HEAD_DIM, (j + 1) * HEAD_DIM)
        stream = res_ref[:, lanes].astype(jnp.float32) + os_[pl.ds(j, rows, stride=heads), :]
        stream_ref[:, lanes] = stream
        squares = squares + stream * stream
        y_ref[:, lanes] = (stream * gain_ref[:, lanes]).astype(jnp.bfloat16)
    hi, mid, low = split3(jnp.sum(squares, axis=1, keepdims=True))
    lane = lax.broadcasted_iota(jnp.int32, (rows, STAT), 1)
    f = lambda v: v.astype(jnp.float32)
    stat = jnp.where(lane == 0, f(hi), jnp.where(lane == 1, f(mid), jnp.where(lane == 2, f(low), 0.0)))
    y_ref[:, width : width + STAT] = stat.astype(jnp.bfloat16)


def attend(me, query, new_keys, new_values, key_cache, value_cache, lengths, residual, gain):
    rows, width = query.shape
    heads = width // HEAD_DIM
    block = 4
    gain = gain.reshape(1, width)
    arrays = (query, new_keys, new_values, key_cache, value_cache, residual, gain)
    in_hbm = [pltpu.with_memory_space_constraint(a, pltpu.HBM) for a in (lengths, *arrays)]
    return pl.pallas_call(
        functools.partial(attend_kernel, block=block),
        in_specs=[SMEM] + [HBM] * len(in_hbm),
        out_specs=[VMEM, VMEM],
        out_shape=[
            jax.ShapeDtypeStruct((rows, width), jnp.float32),
            jax.ShapeDtypeStruct((rows, width + STAT), jnp.bfloat16),
        ],
        scratch_shapes=[pltpu.VMEM(a.shape, a.dtype) for a in arrays]
        + [
            pltpu.SMEM(lengths.shape, lengths.dtype),
            pltpu.VMEM((rows * heads, HEAD_DIM), jnp.float32),
            pltpu.VMEM((rows * heads, HEAD_DIM), jnp.float32),
            pltpu.SemaphoreType.DMA((6,)),
            pltpu.SemaphoreType.DMA((2, rows // block)),
        ],
        compiler_params=pltpu.CompilerParams(vmem_limit_bytes=16 << 20),
        name="attend",
    )(me, *in_hbm)


def first_of(me_ref, place):
    j, n, share, inner = place
    return pl.multiple_of(lax.rem(me_ref[0] + j, n) * share + inner, 16)


def tile_copies(first, weights, tiles, targets, sems, slot=lambda t: t):
    copies = []
    for t in tiles:
        pair = []
        for j, (w, b) in enumerate(zip(weights, targets)):
            count, width = b.shape[1:]
            pair.append(
                pltpu.make_async_copy(
                    w.at[pl.ds(first, count), pl.ds(t * width, width)], b.at[slot(t)], sems.at[j, slot(t)]
                )
            )
        copies.append(pair)
    return copies


def ahead_kernel(me, gate, up, *refs, places):
    outs, sems = refs[: 2 * len(places)], refs[-1]
    copies = []
    for i, place in enumerate(places):
        pair = outs[2 * i : 2 * i + 2]
        steps = pair[0].shape[0]
        copies += tile_copies(first_of(me, place), (gate, up), range(steps), pair, sems.at[i])
    for group in copies:
        for c in group:
            c.start()
    for group in copies:
        for c in group:
            c.wait()


def ahead(me, gate, up, places, counts):
    width = gate.shape[1]
    tile = min(512, width)
    steps = width // tile
    gate, up = (pltpu.with_memory_space_constraint(a, pltpu.HBM) for a in (gate, up))
    outs = pl.pallas_call(
        functools.partial(ahead_kernel, places=places),
        in_specs=[SMEM, HBM, HBM],
        out_specs=[VMEM] * (2 * len(places)),
        out_shape=[pltpu.VMEM((steps, c, tile), jnp.bfloat16) for c in counts for _ in range(2)],
        scratch_shapes=[pltpu.SemaphoreType.DMA((len(places), 2, steps))],
        compiler_params=pltpu.CompilerParams(vmem_limit_bytes=2 << 20),
        cost_estimate=pl.CostEstimate(
            flops=0, bytes_accessed=4 * sum(counts) * width, transcendentals=0
        ),
        name="ahead",
    )(me, gate, up)
    return [tuple(outs[2 * i : 2 * i + 2]) for i in range(len(places))]


def accumulate(i, steps, count, buffers, piece_refs, tile, acc, out):
    x = jnp.concatenate([p[:, i * tile : (i + 1) * tile] for p in piece_refs], axis=0)
    for j, b in enumerate(buffers):
        part = lax.dot_general(b, x, contract_last, preferred_element_type=jnp.float32)
        at = slice(j * count, (j + 1) * count)
        if i > 0:
            part = acc[at] + part
        if i < steps - 1:
            acc[at] = part
        else:
            out[at] = part.astype(out.dtype)


def send_kernel(*refs, pieces, stats):
    piece_refs, refs = refs[:pieces], refs[pieces:]
    gate, up, out, *refs = refs
    acc = refs[-1]
    steps, count, tile = gate.shape
    width = steps * tile
    if stats:
        stat = jnp.concatenate([p[:, width : width + STAT] for p in piece_refs], axis=0)
        stat = stat.astype(jnp.float32).T[:16]
        refs[0][...] = stat
        out[2 * count : 2 * count + 16, :] = stat.astype(out.dtype)
    for i in range(steps):
        accumulate(i, steps, count, (gate[i], up[i]), piece_refs, tile, acc, out)


def send_units(pieces, gate, up, stats):
    rows = sum(p.shape[0] for p in pieces)
    n = len(pieces)
    steps, count, tile = gate.shape
    width = steps * tile
    out_shape = [jax.ShapeDtypeStruct((2 * count + (16 if stats else 0), rows), jnp.bfloat16)]
    if stats:
        out_shape.append(jax.ShapeDtypeStruct((16, rows), jnp.float32))
    return pl.pallas_call(
        functools.partial(send_kernel, pieces=n, stats=stats),
        in_specs=[VMEM] * (n + 2),
        out_specs=[VMEM] * len(out_shape),
        out_shape=out_shape,
        scratch_shapes=[pltpu.VMEM((2 * count, rows), jnp.float32)],
        compiler_params=pltpu.CompilerParams(vmem_limit_bytes=6 << 20),
        cost_estimate=pl.CostEstimate(
            flops=4 * count * width * rows, bytes_accessed=4 * count * width, transcendentals=0
        ),
    )(*pieces, gate, up)


def keep_kernel(*refs, pieces, place, steps, depth):
    me, *refs = refs
    piece_refs, refs = refs[:pieces], refs[pieces:]
    gate, up, out, gbuf, ubuf, sems = refs
    count, tile = gbuf.shape[1:]
    copies = tile_copies(
        first_of(me, place), (gate, up), range(steps), (gbuf, ubuf), sems, lambda t: t % depth
    )
    for group in copies[:depth]:
        for c in group:
            c.start()
    for i in range(steps):
        for c in copies[i]:
            c.wait()
        accumulate(i, steps, count, (gbuf[i % depth], ubuf[i % depth]), piece_refs, tile, out, out)
        if i + depth < steps:
            for c in copies[i + depth]:
                c.start()


def keep_units(me, pieces, gate, up, place, count):
    rows = sum(p.shape[0] for p in pieces)
    n = len(pieces)
    width = gate.shape[1]
    tile = min(512, width)
    steps = width // tile
    depth = min(steps, max(2, (16 << 20) // (4 * count * tile)))
    gate, up = (pltpu.with_memory_space_constraint(a, pltpu.HBM) for a in (gate, up))
    return pl.pallas_call(
        functools.partial(keep_kernel, pieces=n, place=place, steps=steps, depth=depth),
        in_specs=[SMEM] + [VMEM] * n + [HBM] * 2,
        out_specs=VMEM,
        out_shape=jax.ShapeDtypeStruct((2 * count, rows), jnp.float32),
        scratch_shapes=[pltpu.VMEM((depth, count, tile), jnp.bfloat16)] * 2
        + [pltpu.SemaphoreType.DMA((2, depth))],
        compiler_params=pltpu.CompilerParams(vmem_limit_bytes=24 << 20),
        cost_estimate=pl.CostEstimate(
            flops=4 * count * width * rows, bytes_accessed=4 * count * width, transcendentals=0
        ),
    )(me, *pieces, gate, up)


def hidden_kernel(mine, stat_ref, *refs, counts, features, partners):
    *received, out = refs
    total = out.shape[0]
    base = sum(counts[:1])
    stat = stat_ref[...]
    for r in received[:partners]:
        stat = stat + r[2 * base : 2 * base + 16, :].astype(jnp.float32)
    stat = stat[0:1] + stat[1:2] + stat[2:3]
    inverse = lax.rsqrt(stat / features + 1e-05)
    received = received[partners:]
    at = 0
    for k, count in enumerate(counts[1:]):
        gate = mine[at : at + count, :]
        up = mine[total + at : total + at + count, :]
        for r in received[k * partners : (k + 1) * partners]:
            gate = gate + r[:count, :].astype(jnp.float32)
            up = up + r[count : 2 * count, :].astype(jnp.float32)
        out[at : at + count, :] = (jax.nn.silu(gate * inverse) * (up * inverse)).astype(jnp.bfloat16)
        at += count


def hidden_units(mine, stat, first, received, counts, features):
    rows = mine.shape[1]
    partners = len(first)
    chunks = [*first, *(r for group in received for r in group)]
    return pl.pallas_call(
        functools.partial(hidden_kernel, counts=counts, features=features, partners=partners),
        in_specs=[VMEM] * (2 + len(chunks)),
        out_specs=VMEM,
        out_shape=jax.ShapeDtypeStruct((sum(counts[1:]), rows), jnp.bfloat16),
        compiler_params=pltpu.CompilerParams(vmem_limit_bytes=8 << 20),
    )(mine, stat, *chunks)


def down_kernel(me, *refs, parts, tile, has_acc, last, keep, offset, place):
    hidden, refs = refs[:parts], refs[parts:]
    weight, *refs = refs
    if has_acc:
        acc, *refs = refs
    if last:
        send, kept, *refs = refs
    else:
        out, *refs = refs
    turned, buf, sems = refs
    steps, units_in = buf.shape[:2]
    first = first_of(me, place)

    copies = [
        pltpu.make_async_copy(
            weight.at[pl.ds(first, units_in), pl.ds(offset + i * tile, tile)], buf.at[i], sems.at[i]
        )
        for i in range(steps)
    ]
    for c in copies:
        c.start()
    whole = jnp.concatenate([h[...] for h in hidden], axis=0) if parts > 1 else hidden[0][...]
    turned[...] = whole.T
    for i in range(steps):
        copies[i].wait()
        lanes = slice(i * tile, (i + 1) * tile)
        part = jnp.dot(turned[...], buf[i], preferred_element_type=jnp.float32)
        if has_acc:
            part = acc[:, offset + i * tile : offset + (i + 1) * tile] + part
        if last:
            kept[:, lanes] = part[:keep]
            send[:, lanes] = part[keep:].astype(jnp.bfloat16)
        else:
            out[:, lanes] = part


def down(me, place, hidden, weight, acc, keep, offset=0, width=None):
    rows = hidden[0].shape[1]
    width = width or weight.shape[1]
    tile = min(512, width)
    last = keep > 0
    parts = len(hidden)
    total = sum(h.shape[0] for h in hidden)
    if last:
        out_shape = [
            jax.ShapeDtypeStruct((rows - keep, width), jnp.bfloat16),
            jax.ShapeDtypeStruct((keep, width), jnp.float32),
        ]
    else:
        out_shape = jax.ShapeDtypeStruct((rows, width), jnp.float32)
    extra = [] if acc is None else [acc]
    return pl.pallas_call(
        functools.partial(
            down_kernel, parts=parts, tile=tile, has_acc=acc is not None, last=last, keep=keep, offset=offset, place=place
        ),
        in_specs=[SMEM] + [VMEM] * parts + [ANY] + [VMEM] * len(extra),
        out_specs=[VMEM, VMEM] if last else VMEM,
        out_shape=out_shape,
        scratch_shapes=[
            pltpu.VMEM((rows, total), jnp.bfloat16),
            pltpu.VMEM((width // tile, total, tile), jnp.bfloat16),
            pltpu.SemaphoreType.DMA((width // tile,)),
        ],
        compiler_params=pltpu.CompilerParams(vmem_limit_bytes=36 << 20),
        cost_estimate=pl.CostEstimate(
            flops=2 * total * width * rows, bytes_accessed=2 * total * width, transcendentals=0
        ),
    )(me, *hidden, weight, *extra)


def combine_kernel(*refs, near):
    kept, *refs = refs
    received, outs = refs[:near], refs[near:]
    size = outs[0].shape[0]
    for s, out in enumerate(outs):
        at = slice(s * size, (s + 1) * size)
        total = kept[at]
        for r in received:
            total = total + r[at].astype(jnp.float32)
        out[...] = total.astype(out.dtype)


def combine(kept, received, size):
    blocks, width = kept.shape[0] // size, kept.shape[1]
    return pl.pallas_call(
        functools.partial(combine_kernel, near=len(received)),
        in_specs=[VMEM] * (1 + len(received)),
        out_specs=[VMEM] * blocks,
        out_shape=[
            jax.ShapeDtypeStruct((size, width), jnp.bfloat16 if s else jnp.float32) for s in range(blocks)
        ],
        compiler_params=pltpu.CompilerParams(vmem_limit_bytes=24 << 20),
        name="combine",
    )(kept, *received)


def solution(mesh):
    n_req, n_head, n_pair = (mesh.shape[a] for a in ("req", "head", "pair"))

    def shift(x, axis, by):
        n = mesh.shape[axis]
        return lax.ppermute(x, axis, [(i, (i + by) % n) for i in range(n)])

    order = sorted(range(1, n_req), key=lambda s: min(s, n_req - s))

    def local(
        query,
        new_keys,
        new_values,
        key_cache,
        value_cache,
        lengths,
        residual,
        norm_gain,
        gate_weight,
        up_weight,
        down_weight,
    ):
        slot_rows, width = query.shape
        features = width * n_head
        unit_count = gate_weight.shape[0]
        share = unit_count // n_head
        quarter = share // 4
        counts = [quarter, 2 * quarter, quarter] if share % 64 == 0 else [share]
        groups = [[0, 1], [2]] if len(counts) == 3 else [[0]]
        inner = [sum(counts[:k]) for k in range(len(counts))]
        me = lax.axis_index("head").astype(jnp.int32).reshape(1)

        def place(j, k):
            return (j, n_head, share, inner[k])

        stream, y = attend(
            me, query, new_keys, new_values, key_cache, value_cache, lengths, residual, norm_gain
        )
        moved = {s: shift(y, "req", -s) for s in order}
        sends = [(k, j) for k in range(len(counts)) for j in range(1, n_head)]
        have = ahead(
            me, gate_weight, up_weight, [place(j, k) for k, j in sends], [counts[k] for k, _ in sends]
        )
        have = [list(pair) for pair in have]
        *blocks, have[0][0] = lax.optimization_barrier(
            tuple(moved[s] for s in range(1, n_req)) + (have[0][0],)
        )
        near = [y] + blocks
        pieces = list(near)
        for p in range(1, n_pair):
            pieces += [shift(b, "pair", -p) for b in near]
        rows = slot_rows * len(pieces)

        received = [[] for _ in counts]
        for n, (k, j) in enumerate(sends):
            out, *stats = send_units(pieces, *have[n], k == 0)
            if k == 0:
                stat_own = stats[0]
            if n + 1 < len(sends):
                out, have[n + 1][0] = lax.optimization_barrier((out, have[n + 1][0]))
            received[k].append(shift(out, "head", j))
        hidden = []
        turn = me
        for group in groups:
            sizes = [counts[k] for k in group]
            mine = keep_units(turn, pieces, gate_weight, up_weight, place(0, group[0]), sum(sizes))
            hidden.append(
                hidden_units(mine, stat_own, received[0], [received[k] for k in group], [counts[0], *sizes], features)
            )
            hidden[-1], turn = lax.optimization_barrier((hidden[-1], turn))
        others = [[shift(h, "head", j) for h in hidden] for j in range(1, n_head)]

        keep = rows // n_pair
        acc = down(me, place(0, 0), hidden, down_weight, None, 0)
        for j in range(1, n_head - 1):
            acc = down(me, place(n_head - j, 0), others[j - 1], down_weight, acc, 0)
        j = n_head - 1
        cuts = 1
        results = []
        for c in range(cuts):
            size = width // cuts
            send, kept = down(me, place(n_head - j, 0), others[j - 1], down_weight, acc, keep, c * size, size)
            received = [shift(send[(p - 1) * keep : p * keep], "pair", p) for p in range(1, n_pair)]
            blocks = combine(kept, received, slot_rows)
            parts = {s: shift(blocks[s], "req", s) for s in order[::-1]}
            result = stream[:, c * size : (c + 1) * size] + blocks[0]
            for s in range(1, n_req):
                result = result + parts[s].astype(jnp.float32)
            results.append(result.astype(jnp.bfloat16))
        return jnp.concatenate(results, axis=1)

    rows_spec = P(("groups", "req", "pair"), "head")
    return jax.shard_map(
        local,
        mesh=mesh,
        in_specs=(
            rows_spec,
            rows_spec,
            rows_spec,
            P(("groups", "req", "pair"), None, "head"),
            P(("groups", "req", "pair"), None, "head"),
            P(("groups", "req", "pair")),
            rows_spec,
            P("head"),
            P(("req", "pair"), "head"),
            P(("req", "pair"), "head"),
            P(("req", "pair"), "head"),
        ),
        out_specs=rows_spec,
        check_vma=False,
    )
```

```python
import functools
import math

import jax
import jax.numpy as jnp
from jax import lax
from jax.experimental import pallas as pl
from jax.experimental.pallas import tpu as pltpu
from jax.sharding import PartitionSpec as P


HEAD_DIM = 128
GROUP = 16
LOW = -1e30
STAT = 128

contract_last = (((1,), (1,)), ((), ()))
ANY = pl.BlockSpec(memory_space=pl.ANY)
HBM = pl.BlockSpec(memory_space=pltpu.HBM)
VMEM = pl.BlockSpec(memory_space=pltpu.VMEM)
SMEM = pl.BlockSpec(memory_space=pltpu.SMEM)


def split3(v):
    hi = v.astype(jnp.bfloat16)
    rest = v - hi.astype(jnp.float32)
    mid = rest.astype(jnp.bfloat16)
    low = (rest - mid.astype(jnp.float32)).astype(jnp.bfloat16)
    return hi, mid, low


def attend_kernel(
    me_ref, lengths_hbm, q_hbm, nk_hbm, nv_hbm, k_hbm, v_hbm, res_hbm, gain_hbm, stream_ref, y_ref,
    q_ref, nk_ref, nv_ref, kb, vb, res_ref, gain_ref, lengths, qs, os_, small, sems, *, block,
):
    rows, width = q_ref.shape
    heads = width // HEAD_DIM
    cache, lanes_kv = kb.shape[1:]
    kv = lanes_kv // HEAD_DIM
    scale = 1.0 / math.sqrt(HEAD_DIM)
    first = [(lengths_hbm, lengths), (q_hbm, q_ref), (nk_hbm, nk_ref), (nv_hbm, nv_ref)]
    late = [(res_hbm, res_ref), (gain_hbm, gain_ref)]
    smalls = [pltpu.make_async_copy(s, d, small.at[i]) for i, (s, d) in enumerate(first + late)]
    caches = [
        [
            pltpu.make_async_copy(h.at[pl.ds(i * block, block)], d.at[pl.ds(i * block, block)], sems.at[j, i])
            for j, (h, d) in enumerate(((k_hbm, kb), (v_hbm, vb)))
        ]
        for i in range(rows // block)
    ]
    for c in smalls[:4]:
        c.start()
    for pair in caches:
        for c in pair:
            c.start()
    for c in smalls[4:]:
        c.start()
    for c in smalls[:4]:
        c.wait()
    for j in range(heads):
        qs[pl.ds(j, rows, stride=heads), :] = q_ref[:, j * HEAD_DIM : (j + 1) * HEAD_DIM].astype(jnp.float32)

    column = lax.broadcasted_iota(jnp.int32, (1, cache), 1)
    same = (
        lax.broadcasted_iota(jnp.int32, (heads, lanes_kv), 0) // GROUP
        == lax.broadcasted_iota(jnp.int32, (heads, lanes_kv), 1) // HEAD_DIM
    )
    for i in range(rows // block):
        for c in caches[i]:
            c.wait()
        scores = []
        for row in range(i * block, (i + 1) * block):
            q = qs[row * heads : (row + 1) * heads, :]
            q = jnp.where(same, jnp.concatenate([q] * kv, axis=1), 0.0)
            own = jnp.sum(q * nk_ref[row : row + 1, :].astype(jnp.float32), axis=1, keepdims=True) * scale
            s = lax.dot_general(
                q.astype(jnp.bfloat16), kb[row], contract_last, preferred_element_type=jnp.float32
            )
            scores.append((s * scale, own))
        weights = []
        for b, (s, own) in enumerate(scores):
            live = column < lengths[i * block + b]
            s = jnp.where(live, s, LOW)
            top = jnp.maximum(jnp.max(s, axis=1, keepdims=True), own)
            w = jnp.where(live, jnp.exp(s - top), 0.0)
            own_w = jnp.exp(own - top)
            weights.append((w.astype(jnp.bfloat16), own_w, jnp.sum(w, axis=1, keepdims=True) + own_w))
        for b, (w, own_w, total) in enumerate(weights):
            row = i * block + b
            acc = jnp.dot(w, vb[row], preferred_element_type=jnp.float32)
            acc = (acc + own_w * nv_ref[row : row + 1, :].astype(jnp.float32)) / total
            for g in range(kv):
                heads_g = slice(g * GROUP, (g + 1) * GROUP)
                os_[row * heads + g * GROUP : row * heads + (g + 1) * GROUP, :] = acc[
                    heads_g, g * HEAD_DIM : (g + 1) * HEAD_DIM
                ]

    for c in smalls[4:]:
        c.wait()
    squares = jnp.zeros((rows, HEAD_DIM), jnp.float32)
    for j in range(heads):
        lanes = slice(j * HEAD_DIM, (j + 1) * HEAD_DIM)
        stream = res_ref[:, lanes].astype(jnp.float32) + os_[pl.ds(j, rows, stride=heads), :]
        stream_ref[:, lanes] = stream
        squares = squares + stream * stream
        y_ref[:, lanes] = (stream * gain_ref[:, lanes]).astype(jnp.bfloat16)
    hi, mid, low = split3(jnp.sum(squares, axis=1, keepdims=True))
    lane = lax.broadcasted_iota(jnp.int32, (rows, STAT), 1)
    f = lambda v: v.astype(jnp.float32)
    stat = jnp.where(lane == 0, f(hi), jnp.where(lane == 1, f(mid), jnp.where(lane == 2, f(low), 0.0)))
    y_ref[:, width : width + STAT] = stat.astype(jnp.bfloat16)


def attend(me, query, new_keys, new_values, key_cache, value_cache, lengths, residual, gain):
    rows, width = query.shape
    heads = width // HEAD_DIM
    block = 4
    gain = gain.reshape(1, width)
    arrays = (query, new_keys, new_values, key_cache, value_cache, residual, gain)
    in_hbm = [pltpu.with_memory_space_constraint(a, pltpu.HBM) for a in (lengths, *arrays)]
    return pl.pallas_call(
        functools.partial(attend_kernel, block=block),
        in_specs=[SMEM] + [HBM] * len(in_hbm),
        out_specs=[VMEM, VMEM],
        out_shape=[
            jax.ShapeDtypeStruct((rows, width), jnp.float32),
            jax.ShapeDtypeStruct((rows, width + STAT), jnp.bfloat16),
        ],
        scratch_shapes=[pltpu.VMEM(a.shape, a.dtype) for a in arrays]
        + [
            pltpu.SMEM(lengths.shape, lengths.dtype),
            pltpu.VMEM((rows * heads, HEAD_DIM), jnp.float32),
            pltpu.VMEM((rows * heads, HEAD_DIM), jnp.float32),
            pltpu.SemaphoreType.DMA((6,)),
            pltpu.SemaphoreType.DMA((2, rows // block)),
        ],
        compiler_params=pltpu.CompilerParams(vmem_limit_bytes=16 << 20),
        name="attend",
    )(me, *in_hbm)


def first_of(me_ref, place):
    j, n, share, inner = place
    return pl.multiple_of(lax.rem(me_ref[0] + j, n) * share + inner, 16)


def tile_copies(first, weights, tiles, targets, sems, slot=lambda t: t):
    copies = []
    for t in tiles:
        pair = []
        for j, (w, b) in enumerate(zip(weights, targets)):
            count, width = b.shape[1:]
            pair.append(
                pltpu.make_async_copy(
                    w.at[pl.ds(first, count), pl.ds(t * width, width)], b.at[slot(t)], sems.at[j, slot(t)]
                )
            )
        copies.append(pair)
    return copies


def ahead_kernel(me, gate, up, *refs, places):
    outs, sems = refs[: 2 * len(places)], refs[-1]
    copies = []
    for i, place in enumerate(places):
        pair = outs[2 * i : 2 * i + 2]
        steps = pair[0].shape[0]
        copies += tile_copies(first_of(me, place), (gate, up), range(steps), pair, sems.at[i])
    for group in copies:
        for c in group:
            c.start()
    for group in copies:
        for c in group:
            c.wait()


def ahead(me, gate, up, places, counts):
    width = gate.shape[1]
    tile = min(512, width)
    steps = width // tile
    gate, up = (pltpu.with_memory_space_constraint(a, pltpu.HBM) for a in (gate, up))
    outs = pl.pallas_call(
        functools.partial(ahead_kernel, places=places),
        in_specs=[SMEM, HBM, HBM],
        out_specs=[VMEM] * (2 * len(places)),
        out_shape=[pltpu.VMEM((steps, c, tile), jnp.bfloat16) for c in counts for _ in range(2)],
        scratch_shapes=[pltpu.SemaphoreType.DMA((len(places), 2, steps))],
        compiler_params=pltpu.CompilerParams(vmem_limit_bytes=2 << 20),
        cost_estimate=pl.CostEstimate(
            flops=0, bytes_accessed=4 * sum(counts) * width, transcendentals=0
        ),
        name="ahead",
    )(me, gate, up)
    return [tuple(outs[2 * i : 2 * i + 2]) for i in range(len(places))]


def accumulate(i, steps, count, buffers, piece_refs, tile, acc, out):
    x = jnp.concatenate([p[:, i * tile : (i + 1) * tile] for p in piece_refs], axis=0)
    for j, b in enumerate(buffers):
        part = lax.dot_general(b, x, contract_last, preferred_element_type=jnp.float32)
        at = slice(j * count, (j + 1) * count)
        if i > 0:
            part = acc[at] + part
        if i < steps - 1:
            acc[at] = part
        else:
            out[at] = part.astype(out.dtype)


def send_kernel(*refs, pieces, stats):
    piece_refs, refs = refs[:pieces], refs[pieces:]
    gate, up, out, *refs = refs
    acc = refs[-1]
    steps, count, tile = gate.shape
    width = steps * tile
    if stats:
        stat = jnp.concatenate([p[:, width : width + STAT] for p in piece_refs], axis=0)
        stat = stat.astype(jnp.float32).T[:16]
        refs[0][...] = stat
        out[2 * count : 2 * count + 16, :] = stat.astype(out.dtype)
    for i in range(steps):
        accumulate(i, steps, count, (gate[i], up[i]), piece_refs, tile, acc, out)


def send_units(pieces, gate, up, stats):
    rows = sum(p.shape[0] for p in pieces)
    n = len(pieces)
    steps, count, tile = gate.shape
    width = steps * tile
    out_shape = [jax.ShapeDtypeStruct((2 * count + (16 if stats else 0), rows), jnp.bfloat16)]
    if stats:
        out_shape.append(jax.ShapeDtypeStruct((16, rows), jnp.float32))
    return pl.pallas_call(
        functools.partial(send_kernel, pieces=n, stats=stats),
        in_specs=[VMEM] * (n + 2),
        out_specs=[VMEM] * len(out_shape),
        out_shape=out_shape,
        scratch_shapes=[pltpu.VMEM((2 * count, rows), jnp.float32)],
        compiler_params=pltpu.CompilerParams(vmem_limit_bytes=6 << 20),
        cost_estimate=pl.CostEstimate(
            flops=4 * count * width * rows, bytes_accessed=4 * count * width, transcendentals=0
        ),
    )(*pieces, gate, up)


def keep_kernel(*refs, pieces, place, steps, depth):
    me, *refs = refs
    piece_refs, refs = refs[:pieces], refs[pieces:]
    gate, up, out, gbuf, ubuf, sems = refs
    count, tile = gbuf.shape[1:]
    copies = tile_copies(
        first_of(me, place), (gate, up), range(steps), (gbuf, ubuf), sems, lambda t: t % depth
    )
    for group in copies[:depth]:
        for c in group:
            c.start()
    for i in range(steps):
        for c in copies[i]:
            c.wait()
        accumulate(i, steps, count, (gbuf[i % depth], ubuf[i % depth]), piece_refs, tile, out, out)
        if i + depth < steps:
            for c in copies[i + depth]:
                c.start()


def keep_units(me, pieces, gate, up, place, count):
    rows = sum(p.shape[0] for p in pieces)
    n = len(pieces)
    width = gate.shape[1]
    tile = min(512, width)
    steps = width // tile
    depth = min(steps, max(2, (16 << 20) // (4 * count * tile)))
    gate, up = (pltpu.with_memory_space_constraint(a, pltpu.HBM) for a in (gate, up))
    return pl.pallas_call(
        functools.partial(keep_kernel, pieces=n, place=place, steps=steps, depth=depth),
        in_specs=[SMEM] + [VMEM] * n + [HBM] * 2,
        out_specs=VMEM,
        out_shape=jax.ShapeDtypeStruct((2 * count, rows), jnp.float32),
        scratch_shapes=[pltpu.VMEM((depth, count, tile), jnp.bfloat16)] * 2
        + [pltpu.SemaphoreType.DMA((2, depth))],
        compiler_params=pltpu.CompilerParams(vmem_limit_bytes=24 << 20),
        cost_estimate=pl.CostEstimate(
            flops=4 * count * width * rows, bytes_accessed=4 * count * width, transcendentals=0
        ),
    )(me, *pieces, gate, up)


def hidden_kernel(mine, stat_ref, *refs, counts, features, partners):
    *received, out = refs
    total = out.shape[0]
    base = sum(counts[:1])
    stat = stat_ref[...]
    for r in received[:partners]:
        stat = stat + r[2 * base : 2 * base + 16, :].astype(jnp.float32)
    stat = stat[0:1] + stat[1:2] + stat[2:3]
    inverse = lax.rsqrt(stat / features + 1e-05)
    received = received[partners:]
    at = 0
    for k, count in enumerate(counts[1:]):
        gate = mine[at : at + count, :]
        up = mine[total + at : total + at + count, :]
        for r in received[k * partners : (k + 1) * partners]:
            gate = gate + r[:count, :].astype(jnp.float32)
            up = up + r[count : 2 * count, :].astype(jnp.float32)
        out[at : at + count, :] = (jax.nn.silu(gate * inverse) * (up * inverse)).astype(jnp.bfloat16)
        at += count


def hidden_units(mine, stat, first, received, counts, features):
    rows = mine.shape[1]
    partners = len(first)
    chunks = [*first, *(r for group in received for r in group)]
    return pl.pallas_call(
        functools.partial(hidden_kernel, counts=counts, features=features, partners=partners),
        in_specs=[VMEM] * (2 + len(chunks)),
        out_specs=VMEM,
        out_shape=jax.ShapeDtypeStruct((sum(counts[1:]), rows), jnp.bfloat16),
        compiler_params=pltpu.CompilerParams(vmem_limit_bytes=8 << 20),
    )(mine, stat, *chunks)


def down_kernel(me, *refs, parts, tile, has_acc, last, keep, offset, place, ready, following, more):
    hidden, refs = refs[:parts], refs[parts:]
    weight, *refs = refs
    if has_acc:
        acc, *refs = refs
    if ready:
        have, *refs = refs
    if last:
        send, kept, *refs = refs
    else:
        out, *refs = refs
    if more:
        after, *refs = refs
    turned, buf, sems = refs[:3]
    steps, units_in = buf.shape[:2]
    steps += ready
    first = first_of(me, place)

    copies = [
        pltpu.make_async_copy(
            weight.at[pl.ds(first, units_in), pl.ds(offset + i * tile, tile)],
            buf.at[i - ready],
            sems.at[i - ready],
        )
        for i in range(ready, steps)
    ]
    later = []
    if more:
        next_first = first_of(me, following)
        later = [
            pltpu.make_async_copy(
                weight.at[pl.ds(next_first, after.shape[1]), pl.ds(i * tile, tile)], after.at[i], refs[3].at[i]
            )
            for i in range(more)
        ]

    @pl.when(me[0] >= 0)
    def _():
        for c in copies + later:
            c.start()

    whole = jnp.concatenate([h[...] for h in hidden], axis=0) if parts > 1 else hidden[0][...]
    turned[...] = whole.T
    for i in range(steps):
        if i >= ready:
            copies[i - ready].wait()
        tile_w = have[i] if i < ready else buf[i - ready]
        lanes = slice(i * tile, (i + 1) * tile)
        part = jnp.dot(turned[...], tile_w, preferred_element_type=jnp.float32)
        if has_acc:
            part = acc[:, offset + i * tile : offset + (i + 1) * tile] + part
        if last:
            kept[:, lanes] = part[:keep]
            send[:, lanes] = part[keep:].astype(jnp.bfloat16)
        else:
            out[:, lanes] = part
    for c in later:
        c.wait()


def down(me, place, hidden, weight, acc, keep, offset=0, width=None, have=None, following=None, more=0):
    rows = hidden[0].shape[1]
    width = width or weight.shape[1]
    tile = min(512, width)
    last = keep > 0
    parts = len(hidden)
    total = sum(h.shape[0] for h in hidden)
    if last:
        out_shape = [
            jax.ShapeDtypeStruct((rows - keep, width), jnp.bfloat16),
            jax.ShapeDtypeStruct((keep, width), jnp.float32),
        ]
    else:
        out_shape = [jax.ShapeDtypeStruct((rows, width), jnp.float32)]
    if more:
        out_shape = out_shape + [pltpu.VMEM((more, following[2], tile), jnp.bfloat16)]
    ready = 0 if have is None else have.shape[0]
    extra = ([] if acc is None else [acc]) + ([] if have is None else [have])
    return pl.pallas_call(
        functools.partial(
            down_kernel, parts=parts, tile=tile, has_acc=acc is not None, last=last, keep=keep, offset=offset, place=place,
            ready=ready, following=following, more=more,
        ),
        in_specs=[SMEM] + [VMEM] * parts + [ANY] + [VMEM] * len(extra),
        out_specs=[VMEM] * len(out_shape),
        out_shape=out_shape,
        scratch_shapes=[
            pltpu.VMEM((rows, total), jnp.bfloat16),
            pltpu.VMEM((width // tile - ready, total, tile), jnp.bfloat16),
            pltpu.SemaphoreType.DMA((width // tile - ready,)),
        ]
        + ([pltpu.SemaphoreType.DMA((more,))] if more else []),
        compiler_params=pltpu.CompilerParams(vmem_limit_bytes=36 << 20),
        cost_estimate=pl.CostEstimate(
            flops=2 * total * width * rows, bytes_accessed=2 * total * width, transcendentals=0
        ),
    )(me, *hidden, weight, *extra)


def combine_kernel(*refs, near):
    kept, *refs = refs
    received, outs = refs[:near], refs[near:]
    size = outs[0].shape[0]
    for s, out in enumerate(outs):
        at = slice(s * size, (s + 1) * size)
        total = kept[at]
        for r in received:
            total = total + r[at].astype(jnp.float32)
        out[...] = total.astype(out.dtype)


def combine(kept, received, size):
    blocks, width = kept.shape[0] // size, kept.shape[1]
    return pl.pallas_call(
        functools.partial(combine_kernel, near=len(received)),
        in_specs=[VMEM] * (1 + len(received)),
        out_specs=[VMEM] * blocks,
        out_shape=[
            jax.ShapeDtypeStruct((size, width), jnp.bfloat16 if s else jnp.float32) for s in range(blocks)
        ],
        compiler_params=pltpu.CompilerParams(vmem_limit_bytes=24 << 20),
        name="combine",
    )(kept, *received)


def solution(mesh):
    n_req, n_head, n_pair = (mesh.shape[a] for a in ("req", "head", "pair"))

    def shift(x, axis, by):
        n = mesh.shape[axis]
        return lax.ppermute(x, axis, [(i, (i + by) % n) for i in range(n)])

    order = sorted(range(1, n_req), key=lambda s: min(s, n_req - s))

    def local(
        query,
        new_keys,
        new_values,
        key_cache,
        value_cache,
        lengths,
        residual,
        norm_gain,
        gate_weight,
        up_weight,
        down_weight,
    ):
        slot_rows, width = query.shape
        features = width * n_head
        unit_count = gate_weight.shape[0]
        share = unit_count // n_head
        quarter = share // 4
        counts = [quarter, 2 * quarter, quarter] if share % 64 == 0 else [share]
        groups = [[0, 1], [2]] if len(counts) == 3 else [[0]]
        inner = [sum(counts[:k]) for k in range(len(counts))]
        me = lax.axis_index("head").astype(jnp.int32).reshape(1)

        def place(j, k):
            return (j, n_head, share, inner[k])

        stream, y = attend(
            me, query, new_keys, new_values, key_cache, value_cache, lengths, residual, norm_gain
        )
        moved = {s: shift(y, "req", -s) for s in order}
        sends = [(k, j) for k in range(len(counts)) for j in range(1, n_head)]
        have = ahead(
            me, gate_weight, up_weight, [place(j, k) for k, j in sends], [counts[k] for k, _ in sends]
        )
        have = [list(pair) for pair in have]
        *blocks, have[0][0] = lax.optimization_barrier(
            tuple(moved[s] for s in range(1, n_req)) + (have[0][0],)
        )
        near = [y] + blocks
        pieces = list(near)
        for p in range(1, n_pair):
            pieces += [shift(b, "pair", -p) for b in near]
        rows = slot_rows * len(pieces)

        received = [[] for _ in counts]
        for n, (k, j) in enumerate(sends):
            out, *stats = send_units(pieces, *have[n], k == 0)
            if k == 0:
                stat_own = stats[0]
            if n + 1 < len(sends):
                out, have[n + 1][0] = lax.optimization_barrier((out, have[n + 1][0]))
            received[k].append(shift(out, "head", j))
        hidden = []
        turn = me
        for group in groups:
            sizes = [counts[k] for k in group]
            mine = keep_units(turn, pieces, gate_weight, up_weight, place(0, group[0]), sum(sizes))
            hidden.append(
                hidden_units(mine, stat_own, received[0], [received[k] for k in group], [counts[0], *sizes], features)
            )
            hidden[-1], turn = lax.optimization_barrier((hidden[-1], turn))
        others = [[shift(h, "head", j) for h in hidden] for j in range(1, n_head)]

        keep = rows // n_pair
        more = 5 if n_head == 2 and width >= 4096 else 0
        acc, *tail = down(me, place(0, 0), hidden, down_weight, None, 0, following=place(1, 0), more=more)
        for j in range(1, n_head - 1):
            (acc,) = down(me, place(n_head - j, 0), others[j - 1], down_weight, acc, 0)
        j = n_head - 1
        cuts = 1
        results = []
        for c in range(cuts):
            size = width // cuts
            send, kept = down(me, place(n_head - j, 0), others[j - 1], down_weight, acc, keep, c * size, size, *tail)
            received = [shift(send[(p - 1) * keep : p * keep], "pair", p) for p in range(1, n_pair)]
            blocks = combine(kept, received, slot_rows)
            parts = {s: shift(blocks[s], "req", s) for s in order[::-1]}
            result = stream[:, c * size : (c + 1) * size] + blocks[0]
            for s in range(1, n_req):
                result = result + parts[s].astype(jnp.float32)
            results.append(result.astype(jnp.bfloat16))
        return jnp.concatenate(results, axis=1)

    rows_spec = P(("groups", "req", "pair"), "head")
    return jax.shard_map(
        local,
        mesh=mesh,
        in_specs=(
            rows_spec,
            rows_spec,
            rows_spec,
            P(("groups", "req", "pair"), None, "head"),
            P(("groups", "req", "pair"), None, "head"),
            P(("groups", "req", "pair")),
            rows_spec,
            P("head"),
            P(("req", "pair"), "head"),
            P(("req", "pair"), "head"),
            P(("req", "pair"), "head"),
        ),
        out_specs=rows_spec,
        check_vma=False,
    )
```
